256 devices in a mesh: ctx: 32 (over z, x_hi, core), tp: 8 (over y, x_lo).
Axes of the slice: x: 4 (x_hi: 2, x_lo: 2; x = x_hi * 2 + x_lo), y: 4, z: 8, core: 2. Of those that a mesh axis runs over, the one named last changes fastest.
Arguments:
- token_ids: int32 [4096], P('ctx'), may hold values from 0 to 511
- stream_table: bfloat16 [3, 512, 4096], P(None, None, 'tp'), may hold values from -6 to 6
- filters: float32 [256, 128], P('tp'), may hold values from -4 to 4
- proj_qk: bfloat16 [4096, 2, 4096], P(None, None, 'tp'), may hold values from -4 to 4
Outputs:
- attended: bfloat16 [4096, 4096], P('ctx', 'tp')
The draws below stay inside these ranges and needn't reach their ends.
All inputs are finite; a program needn't handle non-finite values.
Results may differ from the reference program's by a relative error of at most 0.01.
Values may be sent and summed in bfloat16 or wider, within the bound.
No kernel may reach another device: no remote copies, remote signals or barrier semaphores. Data moves between devices by JAX's collectives and lax.ppermute only.
A program may use at most 64 MiB of HBM per device.

```python
import math
import jax
import jax.numpy as jnp
import numpy as np
from jax import lax

VOCAB = 512
CH = 4096
HEADS = 32
HEAD = 128
GROUP = 16
FLEN = 128
SPAN = 8
TOK_DEV = 128
TOKENS = 4096
GROUPS = 256


def draw_filters(key, part):
    tau_key, tap_key = jax.random.split(key)
    tau = jnp.exp(jax.random.uniform(tau_key, (GROUPS, 1), jnp.float32, math.log(8.0), math.log(4000.0)))
    lag_value = jnp.arange(FLEN, dtype=jnp.float32)[None, :]
    envelope = jnp.exp(-lag_value / tau)
    normal_size = jnp.sqrt((1.0 - jnp.exp(-2.0 * FLEN / tau)) / (1.0 - jnp.exp(-2.0 / tau)))
    taps = jax.random.truncated_normal(tap_key, -4.0, 4.0, (GROUPS, FLEN), jnp.float32)
    return taps * envelope / normal_size


def draw_proj_qk(key, part):
    query_key, key_key = jax.random.split(key, 2)
    scale = CH ** (-0.5)
    query_part = jax.random.truncated_normal(query_key, -4.0, 4.0, (CH, CH), jnp.float32) * scale
    key_part = jax.random.truncated_normal(key_key, -4.0, 4.0, (CH, CH), jnp.float32) * scale
    return jnp.stack([query_part, key_part], axis=1).astype(jnp.bfloat16)


def touch_ends(array, own_key, least, largest):
    index_at = [jax.random.randint(jax.random.fold_in(own_key, axis), (), 0, length) for axis, length in enumerate(array.shape)]
    longest = array.shape.index(max(array.shape))
    neighbour = index_at[:longest] + [(index_at[longest] + 1) % array.shape[longest]] + index_at[longest + 1:]
    return array.at[tuple(index_at)].set(least).at[tuple(neighbour)].set(largest)


def block_scale(rng, dims, cuts, low, high):
    def one(axis_at, blocks):
        steps = jax.random.uniform(jax.random.fold_in(jax.random.fold_in(rng, 6), axis_at), (blocks,), jnp.float32, low / len(cuts), high / len(cuts))
        return jnp.repeat(jnp.exp(steps), dims[axis_at] // blocks).reshape((-1,) + (1,) * (len(dims) - axis_at - 1))

    gain = one(*cuts[0])
    for cut in cuts[1:]:
        gain = gain * one(*cut)
    return gain


def cumulative_ranks(count, lean):
    loads = [(1 << 20) // math.isqrt(standing ** lean) + 1 for standing in range(1, count + 1)]
    spread = 1 + sum(loads) // (1 << 30)
    return np.cumsum(np.array([max(1, weight // spread) for weight in loads]))


def ranked_ids(key, shape, count, skew):
    grid = cumulative_ranks(count, skew)
    lot = jax.random.randint(jax.random.fold_in(key, 1), shape, 0, int(grid[count - 1]))
    standing = jnp.searchsorted(jnp.asarray(grid, jnp.int32), lot, side="right")
    return jax.random.permutation(jax.random.fold_in(key, 2), count)[standing].astype(jnp.int32)


def centred(key, shape, scale, most, pieces=(), held_as=jnp.bfloat16):
    entries = jax.random.normal(key, shape, jnp.float32) * scale
    if len(pieces) > 0:
        entries = block_scale(key, shape, pieces, -0.22, 0.18) * entries
    return jnp.clip(entries, min=-most, max=most).astype(held_as)


def setup_inputs(seed: int = 0) -> dict:
    key_list = jax.random.split(jax.random.key(seed), 5)
    token_ids = touch_ends(ranked_ids(key_list[0], (TOKENS,), VOCAB, 2), jax.random.fold_in(key_list[0], 3), 0, VOCAB - 1).astype(jnp.int32)
    stream_table = centred(key_list[1], (3, VOCAB, CH), 1.0, 6.0, ((2, 8),))
    filters = draw_filters(jax.random.fold_in(key_list[4], 71), 0)
    proj_qk = draw_proj_qk(jax.random.fold_in(key_list[4], 71), 0)
    return dict(token_ids=token_ids, stream_table=stream_table, filters=filters, proj_qk=proj_qk)


def head_attention(query_block, key_block, value_block, allowed):
    scores = jnp.dot(query_block, key_block.T, preferred_element_type=jnp.float32) * (HEAD ** -0.5)
    scores = jnp.where(allowed, scores, -jnp.inf)
    row_max = jnp.max(scores, axis=1, keepdims=True)
    weights = jnp.where(allowed, jnp.exp(scores - row_max), 0.0)
    row_sum = jnp.sum(weights, axis=1, keepdims=True)
    mixed = jnp.dot(weights.astype(jnp.bfloat16), value_block, preferred_element_type=jnp.float32)
    return mixed / row_sum


def reference(token_ids, stream_table, filters, proj_qk):
    streams = jnp.take(stream_table, token_ids, axis=1)
    post_gate = streams[0].astype(jnp.float32)
    mixed_in = (streams[1].astype(jnp.float32) * streams[2].astype(jnp.float32)).astype(jnp.bfloat16)
    taps = jnp.repeat(filters, GROUP, axis=0)
    padded = jnp.concatenate([jnp.zeros((FLEN - 1, CH), jnp.float32), mixed_in.astype(jnp.float32)], axis=0)

    def add_lag(lag_index, running):
        window = lax.dynamic_slice_in_dim(padded, FLEN - 1 - lag_index, TOKENS, 0)
        column = lax.dynamic_slice_in_dim(taps, lag_index, 1, 1)
        return running + window * column[:, 0][None, :]

    conv = lax.fori_loop(0, FLEN, add_lag, jnp.zeros((TOKENS, CH), jnp.float32))
    gated = (post_gate * conv).astype(jnp.bfloat16)
    queries = jnp.dot(gated, proj_qk[:, 0, :], preferred_element_type=jnp.float32).astype(jnp.bfloat16)
    keys = jnp.dot(gated, proj_qk[:, 1, :], preferred_element_type=jnp.float32).astype(jnp.bfloat16)
    reach = (SPAN - 1) * TOK_DEV
    key_pad = jnp.concatenate([jnp.zeros((reach, CH), jnp.bfloat16), keys], axis=0)
    value_pad = jnp.concatenate([jnp.zeros((reach, CH), jnp.bfloat16), gated], axis=0)

    def one_block(block_index):
        first = (block_index * TOK_DEV).astype(jnp.int32)
        query_block = lax.dynamic_slice_in_dim(queries, first, TOK_DEV, 0).reshape(TOK_DEV, HEADS, HEAD)
        key_block = lax.dynamic_slice_in_dim(key_pad, first, SPAN * TOK_DEV, 0).reshape(SPAN * TOK_DEV, HEADS, HEAD)
        value_block = lax.dynamic_slice_in_dim(value_pad, first, SPAN * TOK_DEV, 0).reshape(SPAN * TOK_DEV, HEADS, HEAD)
        query_pos = first + jnp.arange(TOK_DEV, dtype=jnp.int32)
        key_pos = first - reach + jnp.arange(SPAN * TOK_DEV, dtype=jnp.int32)
        allowed = (key_pos[None, :] >= 0) & (key_pos[None, :] <= query_pos[:, None])

        def one_head(trio):
            return head_attention(trio[0], trio[1], trio[2], allowed)

        per_head = lax.map(one_head, (jnp.transpose(query_block, (1, 0, 2)), jnp.transpose(key_block, (1, 0, 2)), jnp.transpose(value_block, (1, 0, 2))))
        return jnp.transpose(per_head, (1, 0, 2)).reshape(TOK_DEV, CH)

    blocks_out = lax.map(one_block, jnp.arange(TOKENS // TOK_DEV, dtype=jnp.int32))
    return blocks_out.reshape(TOKENS, CH).astype(jnp.bfloat16)
```

```python
import functools

import jax
import jax.numpy as jnp
from jax import lax
from jax.experimental import pallas as pl
from jax.experimental.pallas import tpu as pltpu
from jax.sharding import PartitionSpec as P

HEAD = 128
GROUP = 16
FLEN = 128
SPAN = 8
TOK = 128
F32 = jnp.float32
BF16 = jnp.bfloat16


VMEM = pl.BlockSpec(memory_space=pltpu.VMEM)


def call(body, out_shape, flops, moved, limit=None):
    one = not isinstance(out_shape, (list, tuple))
    return pl.pallas_call(
        body,
        out_shape=out_shape,
        out_specs=VMEM if one else [VMEM] * len(out_shape),
        compiler_params=pltpu.CompilerParams(vmem_limit_bytes=limit),
        cost_estimate=pl.CostEstimate(flops=flops, bytes_accessed=moved, transcendentals=0),
    )


def dot(a, b, ca=1, cb=0):
    return lax.dot_general(a, b, (((ca,), (cb,)), ((), ())), preferred_element_type=F32)


def onehot(ids_row, vocab):
    column = jnp.transpose(jnp.broadcast_to(ids_row, (TOK, TOK)))
    lane = lax.broadcasted_iota(jnp.int32, (TOK, TOK), 1)
    parts = [(column == lane + k * TOK).astype(F32).astype(BF16) for k in range(vocab // TOK)]
    return jnp.concatenate(parts, axis=1)


def pre_body(ids_ref, table_ref, filters_ref, taps_ref, mixed_ref, post_ref):
    groups = filters_ref.shape[0]
    taps = filters_ref[...]
    high = taps.astype(BF16)
    low = (taps - high.astype(F32)).astype(BF16)
    flip = (
        lax.broadcasted_iota(jnp.int32, (FLEN, FLEN), 0) + lax.broadcasted_iota(jnp.int32, (FLEN, FLEN), 1)
        == FLEN - 1
    ).astype(F32).astype(BF16)
    zeros = jnp.zeros((groups, FLEN), F32)
    for part, value in enumerate((high, low)):
        row = jnp.concatenate([dot(value, flip), zeros], axis=1)
        for g in range(groups):
            spread = jnp.broadcast_to(row[g : g + 1], (FLEN, 2 * FLEN))
            rolled = pltpu.roll(spread, 1, 1, stride=1, stride_axis=0)
            taps_ref[g, :, part * 2 * FLEN : (part + 1) * 2 * FLEN] = rolled.astype(BF16)
    here = onehot(ids_ref[...], table_ref.shape[1])
    mixed_ref[...] = (dot(here, table_ref[1]) * dot(here, table_ref[2])).astype(BF16)
    post_ref[...] = dot(here, table_ref[0]).astype(BF16)


def gate_body(ids_ref, table_ref, taps_ref, mixed_ref, post_ref, gated_ref):
    width = mixed_ref.shape[1]
    before = onehot(ids_ref[...], table_ref.shape[1])
    halo = dot(before, table_ref[1]) * dot(before, table_ref[2])
    halo = jnp.where(lax.axis_index("ctx") > 0, halo, 0.0).astype(BF16)
    both = jnp.concatenate([halo, mixed_ref[...]], axis=0)
    lane_group = lax.broadcasted_iota(jnp.int32, (TOK, HEAD), 1) // GROUP
    per = HEAD // GROUP
    for part in range(width // HEAD):
        cols = slice(part * HEAD, (part + 1) * HEAD)
        window = both[:, cols]
        window = jnp.concatenate([window, window], axis=0)
        conv = jnp.zeros((TOK, HEAD), F32)
        for g in range(per):
            conv = jnp.where(lane_group == g, dot(taps_ref[part * per + g], window), conv)
        gated_ref[:, cols] = (post_ref[:, cols].astype(F32) * conv).astype(BF16)


def window_body(ids_ref, table_ref, taps_ref, value_ref, mixed_t, post_t):
    width = table_ref.shape[2]
    position = lax.axis_index("ctx")
    for n in range(SPAN):
        here = onehot(ids_ref[n : n + 1], table_ref.shape[1])
        mixed = dot(here, table_ref[1]) * dot(here, table_ref[2])
        mixed = jnp.where(position >= SPAN - n, mixed, 0.0).astype(BF16)
        mixed_t[:, n * TOK : (n + 1) * TOK] = jnp.transpose(mixed)
        if n > 0:
            post_t[:, (n - 1) * TOK : n * TOK] = jnp.transpose(dot(here, table_ref[0]).astype(BF16))
    for g in range(width // GROUP):
        rows = slice(g * GROUP, (g + 1) * GROUP)
        windows = jnp.concatenate(
            [mixed_t[rows, n * TOK : (n + 2) * TOK] for n in range(SPAN - 1)], axis=0
        )
        windows = jnp.concatenate([windows, windows], axis=1)
        conv = dot(windows, taps_ref[g], 1, 1)
        for n in range(SPAN - 1):
            post = post_t[rows, n * TOK : (n + 1) * TOK].astype(F32)
            value_ref[SPAN - 2 - n, rows, :] = (post * conv[n * GROUP : (n + 1) * GROUP]).astype(BF16)


def project_body(*refs):
    pieces, weight_ref, query_ref, key_ref = refs[:-3], refs[-3], refs[-2], refs[-1]
    own = lax.axis_index("tp")
    count = len(pieces)
    width = query_ref.shape[1]
    total = None
    for d in range(count):
        part = dot(pieces[d][...], weight_ref[lax.rem(own - d + count, count)])
        total = part if total is None else total + part
    query_ref[...] = total[:, :width].astype(BF16)
    key_ref[...] = total[:, width:].astype(BF16)


def attend_body(query_ref, own_key, own_value, k2, k4, k6, kx, swapped, value_ref, out_ref):
    position = lax.axis_index("ctx")
    odd = lax.rem(position, 2)
    far = [2, 4, 6, 7 - 6 * odd, 1 + 2 * odd, 3 + 2 * odd, 5 + 2 * odd]
    row = lax.broadcasted_iota(jnp.int32, (TOK, TOK), 0)
    col = lax.broadcasted_iota(jnp.int32, (TOK, TOK), 1)
    for h in range(query_ref.shape[1] // HEAD):
        cols = slice(h * HEAD, (h + 1) * HEAD)
        query = query_ref[:, cols]
        keys = [own_key[:, cols], k2[:, cols], k4[:, cols], k6[:, cols], kx[:, cols]]
        keys += [swapped[j, :, cols] for j in range(3)]
        scores = []
        for j, key in enumerate(keys):
            one = dot(query, key, 1, 1) * HEAD ** (-0.5)
            allowed = (col <= row) if j == 0 else (col >= 0) & (position >= far[j - 1])
            scores.append(jnp.where(allowed, one, -1e30))
        scores = jnp.concatenate(scores, axis=1)
        largest = jnp.max(scores, axis=1, keepdims=True)
        weights = jnp.exp(scores - largest)
        weights = jnp.where(scores > -1e29, weights, 0.0)
        row_sum = jnp.sum(weights, axis=1, keepdims=True)
        rounded = weights.astype(BF16)
        total = dot(rounded[:, :TOK], own_value[:, cols])
        for j in range(1, SPAN):
            total += dot(rounded[:, j * TOK : (j + 1) * TOK], value_ref[far[j - 1] - 1, cols, :], 1, 1)
        out_ref[:, cols] = (total / row_sum).astype(BF16)


def behind(value, steps):
    count = lax.axis_size("ctx")
    return lax.ppermute(value, "ctx", [(s, s + steps) for s in range(count - steps)])


def shards(token_ids, stream_table, filters, proj_qk):
    width = stream_table.shape[2]
    groups = filters.shape[0]
    count = lax.axis_size("ctx")
    heads_axis = lax.axis_size("tp")
    shape = jax.ShapeDtypeStruct
    ids = token_ids.reshape(1, TOK)
    back1 = behind(ids, 1)
    taps, mixed, post = call(
        pre_body,
        [shape((groups, FLEN, 4 * FLEN), BF16), shape((TOK, width), BF16), shape((TOK, width), BF16)],
        10**9, 6 * 2**20,
    )(ids, stream_table, filters)
    gated = call(gate_body, shape((TOK, width), BF16), 10**9, 6 * 2**20)(
        back1, stream_table, taps, mixed, post
    )
    pieces = [gated] + [
        lax.ppermute(gated, "tp", [(s, (s + d) % heads_axis) for s in range(heads_axis)])
        for d in range(1, heads_axis)
    ]
    two = jnp.concatenate([back1, ids], axis=0)
    four = jnp.concatenate([behind(two, 2), two], axis=0)
    seven = jnp.concatenate([behind(ids, 8), behind(four, 4), four[:3]], axis=0)
    values = pl.pallas_call(
        window_body,
        out_shape=shape((SPAN - 1, width, TOK), BF16),
        out_specs=VMEM,
        scratch_shapes=[pltpu.VMEM((width, SPAN * TOK), BF16), pltpu.VMEM((width, (SPAN - 1) * TOK), BF16)],
        cost_estimate=pl.CostEstimate(flops=4 * 10**9, bytes_accessed=6 * 2**20, transcendentals=0),
    )(seven, stream_table, taps)
    weights = proj_qk.reshape(heads_axis, width, 2 * width)
    query, key = call(project_body, [shape((TOK, width), BF16)] * 2, 10**9, 10 * 2**20)(*pieces, weights)
    cross = [(s, s + 1) if s % 2 == 0 else (s, s + 7) for s in range(count)]
    keyx = lax.ppermute(key, "ctx", [pair for pair in cross if pair[1] < count])
    k2, k4, k6 = behind(key, 2), behind(key, 4), behind(key, 6)
    swapped = lax.ppermute(jnp.stack([k2, k4, k6]), "ctx", [(s, s ^ 1) for s in range(count)])
    return call(attend_body, shape((TOK, width), BF16), 10**9, 2 * 2**20)(
        query, key, gated, k2, k4, k6, keyx, swapped, values
    )


def solution(mesh):
    placed = (P("ctx"), P(None, None, "tp"), P("tp", None), P(None, None, "tp"))
    return jax.shard_map(
        shards, mesh=mesh, in_specs=placed, out_specs=P("ctx", "tp"), check_vma=False
    )
```

```python
import functools

import jax
import jax.numpy as jnp
from jax import lax
from jax.experimental import pallas as pl
from jax.experimental.pallas import tpu as pltpu
from jax.sharding import PartitionSpec as P

HEAD = 128
GROUP = 16
FLEN = 128
SPAN = 8
TOK = 128
F32 = jnp.float32
BF16 = jnp.bfloat16


PLACES = ((0, 0), (0, 1), (2, 0), (1, 0), (1, 1), (3, 0), (3, 1), (2, 1))
LOADS = ((0,), (1,), (2, 3, 4, 5, 6, 7))
LIMIT = 12 * 2**20
VMEM = pl.BlockSpec(memory_space=pltpu.VMEM)
FAR = pl.BlockSpec(memory_space=pl.ANY)


def call(body, out_shape, flops, moved, limit=None):
    one = not isinstance(out_shape, (list, tuple))
    return pl.pallas_call(
        body,
        out_shape=out_shape,
        out_specs=VMEM if one else [VMEM] * len(out_shape),
        compiler_params=pltpu.CompilerParams(vmem_limit_bytes=limit),
        cost_estimate=pl.CostEstimate(flops=flops, bytes_accessed=moved, transcendentals=0),
    )


def dot(a, b, ca=1, cb=0):
    return lax.dot_general(a, b, (((ca,), (cb,)), ((), ())), preferred_element_type=F32)


def onehot(ids_row, vocab):
    column = jnp.transpose(jnp.broadcast_to(ids_row, (TOK, TOK)))
    lane = lax.broadcasted_iota(jnp.int32, (TOK, TOK), 1)
    parts = [(column == lane + k * TOK).astype(F32).astype(BF16) for k in range(vocab // TOK)]
    return jnp.concatenate(parts, axis=1)


def place_of(k):
    along, flip = PLACES[k]
    tp = lax.axis_index("tp")
    return lax.rem(lax.div(tp, 2) + 4 - along, 4) * 2 + lax.rem(tp + flip, 2)


def load_weights(step, weight_hbm, weight_ref, sems):
    channels = weight_ref.shape[1]
    copies = []
    for j, k in enumerate(LOADS[step]):
        here = pl.ds(pl.multiple_of(place_of(k) * channels, channels), channels)
        copies.append(pltpu.make_async_copy(weight_hbm.at[here], weight_ref.at[j], sems.at[j]))
        copies[-1].start()
    return copies


def taps_body(ids_hbm, filters_hbm, table_hbm, weight_hbm, taps_ref, table_ref, ids_ref, weight_ref, filters_ref, sems, weight_sems):
    filters_copy = pltpu.make_async_copy(filters_hbm, filters_ref, sems.at[0])
    ids_copy = pltpu.make_async_copy(ids_hbm, ids_ref, sems.at[1])
    table_copy = pltpu.make_async_copy(table_hbm, table_ref, sems.at[2])
    filters_copy.start()
    ids_copy.start()
    table_copy.start()
    copies = load_weights(0, weight_hbm, weight_ref, weight_sems)
    row = lax.broadcasted_iota(jnp.int32, (FLEN, FLEN), 0)
    col = lax.broadcasted_iota(jnp.int32, (FLEN, FLEN), 1)
    flip = (((row + col) & (FLEN - 1)) == 0).astype(F32).astype(BF16)
    own = col <= row
    filters_copy.wait()
    taps = filters_ref[...]
    high = taps.astype(BF16)
    low = (taps - high.astype(F32)).astype(BF16)
    turned = dot(high, flip) + dot(low, flip)
    for g in range(taps.shape[0]):
        spread = jnp.broadcast_to(turned[g : g + 1], (FLEN, FLEN))
        circle = pltpu.roll(spread, 0, 1, stride=1, stride_axis=0)
        for part in range(2):
            rounded = circle.astype(BF16).astype(F32)
            base = part * 2 * FLEN
            taps_ref[g, :, base : base + FLEN] = jnp.where(own, 0.0, rounded).astype(BF16)
            taps_ref[g, :, base + FLEN : base + 2 * FLEN] = jnp.where(own, rounded, 0.0).astype(BF16)
            circle = circle - rounded
    for copy in [ids_copy, table_copy] + copies:
        copy.wait()


def gate_body(own_ref, before_ref, table_ref, taps_ref, weight_hbm, gated_ref, pair_ref, weight_ref, sems):
    copies = load_weights(1, weight_hbm, weight_ref, sems)
    pair_ref[0:1] = before_ref[...]
    pair_ref[1:2] = own_ref[...]
    width = table_ref.shape[2]
    vocab = table_ref.shape[1]
    here = onehot(own_ref[...], vocab)
    both = jnp.concatenate([onehot(before_ref[...], vocab), here], axis=0)
    mixed = dot(both, table_ref[1]) * dot(both, table_ref[2])
    row = lax.broadcasted_iota(jnp.int32, mixed.shape, 0)
    mixed = jnp.where((row >= TOK) | (lax.axis_index("ctx") > 0), mixed, 0.0).astype(BF16)
    post = dot(here, table_ref[0])
    lane_group = lax.broadcasted_iota(jnp.int32, (TOK, HEAD), 1) // GROUP
    per = HEAD // GROUP
    for part in range(width // HEAD):
        cols = slice(part * HEAD, (part + 1) * HEAD)
        window = jnp.concatenate([mixed[:, cols], mixed[:, cols]], axis=0)
        taps = taps_ref[part * per : (part + 1) * per].reshape(per * FLEN, 4 * FLEN)
        every = dot(taps, window)
        conv = every[:TOK]
        for g in range(1, per):
            conv = jnp.where(lane_group == g, every[g * TOK : (g + 1) * TOK], conv)
        gated_ref[:, cols] = (post[:, cols] * conv).astype(BF16)
    for copy in copies:
        copy.wait()


def decode(tail, before):
    code = tail.astype(F32)[:1, before * 2 * TOK : (before + 1) * 2 * TOK]
    return code[:, :TOK] * 16.0 + code[:, TOK:]


def window_values(rows, nearest, table_ref, taps_ref, value_ref, mixed_t, post_t, prepare=None):
    vocab, width = table_ref.shape[1], table_ref.shape[2]
    many = len(rows) - 1
    position = lax.axis_index("ctx")
    entry = lax.broadcasted_iota(jnp.int32, (vocab, TOK), 0).astype(F32)
    here = [(entry == jnp.broadcast_to(row, entry.shape)).astype(F32).astype(BF16) for row in rows]
    every = jnp.concatenate(here, axis=1)
    mixed = dot(table_ref[1], every, 0, 0) * dot(table_ref[2], every, 0, 0)
    for n in range(many + 1):
        part = mixed[:, n * TOK : (n + 1) * TOK]
        mixed_t[:, n * TOK : (n + 1) * TOK] = jnp.where(position >= nearest + many - n, part, 0.0).astype(BF16)
    post_t[...] = dot(table_ref[0], jnp.concatenate(here[1:], axis=1), 0, 0).astype(BF16)
    if prepare is not None:
        prepare()
    for g in range(width // GROUP):
        rows = slice(g * GROUP, (g + 1) * GROUP)
        windows = jnp.concatenate([mixed_t[rows, n * TOK : (n + 2) * TOK] for n in range(many)], axis=0)
        conv = dot(windows, taps_ref[g], 1, 1)
        for n in range(many):
            post = post_t[rows, n * TOK : (n + 1) * TOK].astype(F32)
            value_ref[many - 1 - n, rows, :] = (post * conv[n * GROUP : (n + 1) * GROUP]).astype(BF16)


def attend(query, keys, values, allowed):
    scores = dot(query, jnp.concatenate(keys, axis=0), 1, 1) * HEAD ** (-0.5)
    scores = jnp.where(allowed, scores, -1e30)
    largest = jnp.max(scores, axis=1, keepdims=True)
    weights = jnp.where(allowed, jnp.exp(scores - largest), 0.0)
    rounded = weights.astype(BF16)
    first = len(keys) - len(values)
    total = dot(rounded[:, first * TOK :], jnp.concatenate(values, axis=1), 1, 1)
    return largest, jnp.sum(weights, axis=1, keepdims=True), total, rounded


def masks(far, own):
    row = lax.broadcasted_iota(jnp.int32, (TOK, TOK), 0)
    col = lax.broadcasted_iota(jnp.int32, (TOK, TOK), 1)
    position = lax.axis_index("ctx")
    allowed = ([col <= row] if own else []) + [(col >= 0) & (position >= d) for d in far]
    return jnp.concatenate([a.astype(F32) for a in allowed], axis=1) > 0.5


def near_body(
    query_ref, own_key, own_value, pair, k2, k4, near, table, filters_hbm,
    value_ref, total_ref, stat_ref, taps_ref, mixed_t, post_t, filters_ref, sem,
):
    filters_copy = pltpu.make_async_copy(filters_hbm, filters_ref, sem)
    filters_copy.start()
    odd = lax.rem(lax.axis_index("ctx"), 2)

    def prepare():
        filters_copy.wait()
        row = lax.broadcasted_iota(jnp.int32, (FLEN, FLEN), 0)
        col = lax.broadcasted_iota(jnp.int32, (FLEN, FLEN), 1)
        flip = (((row + col) & (FLEN - 1)) == 0).astype(F32).astype(BF16)
        turned = dot(filters_ref[...].astype(BF16), flip)
        for g in range(taps_ref.shape[0]):
            spread = jnp.broadcast_to(turned[g : g + 1], (FLEN, FLEN))
            circle = pltpu.roll(spread, 0, 1, stride=1, stride_axis=0)
            taps_ref[g, :, :FLEN] = jnp.where(col <= row, 0.0, circle).astype(BF16)
            taps_ref[g, :, FLEN:] = jnp.where(col <= row, circle, 0.0).astype(BF16)

    rows = [decode(k4[TOK:, :], 1), decode(k4[TOK:, :], 0), decode(k2[TOK:, :], 1), decode(k2[TOK:, :], 0)]
    window_values(rows + [pair[0:1].astype(F32)], 1, table, taps_ref, value_ref, mixed_t, post_t, prepare)
    far = [2, 4, 1 + 2 * odd]
    allowed = masks(far, True)
    for h in range(query_ref.shape[1] // HEAD):
        cols = slice(h * HEAD, (h + 1) * HEAD)
        keys = [own_key[:TOK, cols], k2[:TOK, cols], k4[:TOK, cols], near[0, :TOK, cols]]
        largest, row_sum, total, rounded = attend(
            query_ref[:, cols], keys, [value_ref[d - 1, cols, :] for d in far], allowed
        )
        total_ref[:, cols] = total + dot(rounded[:, :TOK], own_value[:, cols])
        stat_ref[2 * h] = jnp.broadcast_to(largest, (TOK, HEAD))
        stat_ref[2 * h + 1] = jnp.broadcast_to(row_sum, (TOK, HEAD))


def values_body(k4, k6, up2, near, table, taps, value_ref, mixed_t, post_t):
    odd = lax.rem(lax.axis_index("ctx"), 2) == 1
    last = jnp.where(odd, decode(up2[TOK:, :], 0), decode(near[2, TOK:, :], 1))
    rows = [last, decode(k6[TOK:, :], 1), decode(k6[TOK:, :], 0), decode(k4[TOK:, :], 1)]
    window_values(rows, 5, table, taps, value_ref, mixed_t, post_t)


def far_body(query_ref, k6, near, near6, near_value, far_value, total_ref, stat_ref, out_ref, value_ref):
    odd = lax.rem(lax.axis_index("ctx"), 2)
    far = [6, 3 + 2 * odd, 7 - 6 * odd, 5 + 2 * odd]
    value_ref[:4] = near_value[...]
    value_ref[4:] = far_value[...]
    allowed = masks(far, False)
    for h in range(query_ref.shape[1] // HEAD):
        cols = slice(h * HEAD, (h + 1) * HEAD)
        keys = [k6[:TOK, cols], near[1, :TOK, cols], near[2, :TOK, cols], near6[:TOK, cols]]
        largest, row_sum, total, _ = attend(
            query_ref[:, cols], keys, [value_ref[d - 1, cols, :] for d in far], allowed
        )
        before, before_sum = stat_ref[2 * h], stat_ref[2 * h + 1]
        most = jnp.maximum(before, largest)
        scale, before_scale = jnp.exp(largest - most), jnp.exp(before - most)
        numerator = total * scale + total_ref[:, cols] * before_scale
        out_ref[:, cols] = (numerator / (row_sum * scale + before_sum * before_scale)).astype(BF16)


def term_of(piece, weight):
    channels = piece.shape[1]
    row = lax.broadcasted_iota(jnp.int32, (HEAD, 2 * HEAD), 0)
    col = lax.broadcasted_iota(jnp.int32, (HEAD, 2 * HEAD), 1)
    halves = []
    for which in range(2):
        place = (col == 2 * row + which).astype(F32).astype(BF16)
        parts = [dot(piece[:, j * HEAD : (j + 1) * HEAD], place).astype(BF16) for j in range(channels // HEAD)]
        halves.append(jnp.concatenate(parts, axis=1))
    return dot(jnp.concatenate(halves, axis=0), weight.reshape(2 * channels, weight.shape[2]))


def own_body(piece, own_weight, weight_hbm, weight_ref, total_ref, sems):
    copies = load_weights(2, weight_hbm, weight_ref, sems)
    total_ref[...] = term_of(piece[...], own_weight[0])
    for copy in copies:
        copy.wait()


def project_body(chosen, last, *refs):
    count, loads = len(chosen), len(LOADS)
    arrays, weights, total_ref, refs = refs[:count], refs[count : count + loads], refs[count + loads], refs[count + loads + 1 :]
    total = total_ref[...]
    for numbers, array in zip(chosen, arrays):
        for j, k in enumerate(numbers):
            step = [k in load for load in LOADS].index(True)
            piece = array[...] if len(numbers) == 1 else array[j]
            total = total + term_of(piece, weights[step][LOADS[step].index(k)])
    if not last:
        refs[0][...] = total
        return
    pair_ref, query_ref, key_ref = refs
    rows, width = query_ref.shape
    query_ref[...] = total[:rows].astype(BF16)
    key_ref[:rows] = total[rows:].astype(BF16)
    ids = [pair_ref[1:2], pair_ref[0:1]]
    code = jnp.concatenate([part for row in ids for part in (row >> 4, row & 15)], axis=1).astype(F32)
    key_ref[rows:] = jnp.broadcast_to(code, (key_ref.shape[0] - rows, width)).astype(BF16)


def behind(value, steps):
    count = lax.axis_size("ctx")
    return lax.ppermute(value, "ctx", [(s, s + steps) for s in range(count - steps)])


def shards(token_ids, stream_table, filters, proj_qk):
    width = stream_table.shape[2]
    groups = filters.shape[0]
    count = lax.axis_size("ctx")
    heads_axis = lax.axis_size("tp")
    shape = jax.ShapeDtypeStruct
    ids = token_ids.reshape(1, TOK)
    back1 = behind(ids, 1)
    weight_hbm = pltpu.with_memory_space_constraint(proj_qk, pltpu.MemorySpace.HBM)
    sizes = [shape((len(load), width) + proj_qk.shape[1:], BF16) for load in LOADS]
    sems = [pltpu.SemaphoreType.DMA((len(load),)) for load in LOADS]
    params = pltpu.CompilerParams(vmem_limit_bytes=LIMIT)
    taps, table, ids_near, weight0 = pl.pallas_call(
        taps_body,
        out_shape=[
            shape((groups, FLEN, 4 * FLEN), BF16), shape(stream_table.shape, BF16), shape(ids.shape, jnp.int32), sizes[0],
        ],
        in_specs=[FAR] * 4,
        out_specs=[VMEM] * 4,
        scratch_shapes=[pltpu.VMEM(filters.shape, F32), pltpu.SemaphoreType.DMA((3,)), sems[0]],
        compiler_params=params,
        cost_estimate=pl.CostEstimate(flops=10**8, bytes_accessed=4 * 2**20, transcendentals=0),
    )(*[pltpu.with_memory_space_constraint(a, pltpu.MemorySpace.HBM) for a in (ids, filters, stream_table)], weight_hbm)
    gated, pair, weight1 = pl.pallas_call(
        gate_body,
        out_shape=[shape((TOK, width), BF16), shape((2, TOK), jnp.int32), sizes[1]],
        in_specs=[VMEM] * 4 + [FAR],
        out_specs=[VMEM] * 3,
        scratch_shapes=[sems[1]],
        compiler_params=params,
        cost_estimate=pl.CostEstimate(flops=10**9, bytes_accessed=4 * 2**20, transcendentals=0),
    )(ids_near, back1, table, taps, weight_hbm)

    def spread(value, along, flip):
        route = [(s, (s // 2 + along) % 4 * 2 + (s + flip) % 2) for s in range(heads_axis)]
        return lax.ppermute(value, "tp", route)

    flipped = spread(gated, 0, 1)
    far = spread(gated, 2, 0)
    weight2, total = pl.pallas_call(
        own_body,
        out_shape=[sizes[2], shape((2 * TOK, width), F32)],
        in_specs=[VMEM, VMEM, FAR],
        out_specs=[VMEM] * 2,
        scratch_shapes=[sems[2]],
        compiler_params=params,
        cost_estimate=pl.CostEstimate(flops=10**9, bytes_accessed=2 * 2**20, transcendentals=0),
    )(gated, weight0, weight_hbm)
    flipped, total = lax.optimization_barrier((flipped, total))
    both = jnp.stack([gated, flipped])
    up = spread(both, 1, 0)
    down = spread(both, 3, 0)
    farflip = spread(flipped, 2, 0)
    weights = [weight0, weight1, weight2]
    total = call(
        functools.partial(project_body, ((1,), (2,)), False), shape(total.shape, F32), 10**9, 2**20, LIMIT
    )(flipped, far, *weights, total)
    total = call(
        functools.partial(project_body, ((3, 4), (5, 6)), False), shape(total.shape, F32), 2 * 10**9, 2**20, LIMIT
    )(up, down, *weights, total)
    query, key = call(
        functools.partial(project_body, ((7,),), True),
        [shape((TOK, width), BF16), shape((TOK + 8, width), BF16)], 10**9, 2**20, LIMIT,
    )(farflip, *weights, total, pair)
    position = lax.axis_index("ctx")
    lower, odd = position % 4 < 2, position % 2 == 1
    cross = lax.ppermute(key, "ctx", [(s, s ^ 2) for s in range(count)])
    up1 = behind(key, 4)
    up1x = behind(cross, 4)
    up2 = lax.ppermute(up1, "ctx", [(s, s + 4) for s in range(count - 4) if s % 2 == 1])
    up2x = lax.ppermute(up1x, "ctx", [(s, s + 4) for s in range(count - 4) if s % 4 < 2])
    k2, k4, k6 = jnp.where(lower, up1x, cross), up1, jnp.where(lower, up2x, up1x)
    swap = [(s, s ^ 1) for s in range(count)]
    near = lax.ppermute(jnp.stack([k2, k4, jnp.where(odd, up2, key)]), "ctx", swap)
    near6 = lax.ppermute(k6, "ctx", swap)
    heads = width // HEAD
    near_value, total, stat, taps = pl.pallas_call(
        near_body,
        out_shape=[
            shape((4, width, TOK), BF16), shape((TOK, width), F32), shape((2 * heads, TOK, HEAD), F32),
            shape((groups, FLEN, 2 * FLEN), BF16),
        ],
        in_specs=[VMEM] * 8 + [FAR],
        out_specs=[VMEM] * 4,
        scratch_shapes=[
            pltpu.VMEM((width, 5 * TOK), BF16), pltpu.VMEM((width, 4 * TOK), BF16), pltpu.VMEM(filters.shape, F32),
            pltpu.SemaphoreType.DMA,
        ],
        compiler_params=params,
        cost_estimate=pl.CostEstimate(flops=3 * 10**9, bytes_accessed=6 * 2**20, transcendentals=0),
    )(query, key, gated, pair, k2, k4, near, table, pltpu.with_memory_space_constraint(filters, pltpu.MemorySpace.HBM))
    far_value = pl.pallas_call(
        values_body,
        out_shape=shape((3, width, TOK), BF16),
        out_specs=VMEM,
        scratch_shapes=[pltpu.VMEM((width, 4 * TOK), BF16), pltpu.VMEM((width, 3 * TOK), BF16)],
        compiler_params=params,
        cost_estimate=pl.CostEstimate(flops=2 * 10**9, bytes_accessed=6 * 2**20, transcendentals=0),
    )(k4, k6, up2, near, table, taps)
    return pl.pallas_call(
        far_body,
        out_shape=shape((TOK, width), BF16),
        out_specs=VMEM,
        scratch_shapes=[pltpu.VMEM((SPAN - 1, width, TOK), BF16)],
        compiler_params=params,
        cost_estimate=pl.CostEstimate(flops=10**9, bytes_accessed=6 * 2**20, transcendentals=0),
    )(query, k6, near, near6, near_value, far_value, total, stat)


def solution(mesh):
    placed = (P("ctx"), P(None, None, "tp"), P("tp", None), P(None, None, "tp"))

    return jax.shard_map(shards, mesh=mesh, in_specs=placed, out_specs=P("ctx", "tp"), check_vma=False)
```

```python
import functools

import jax
import jax.numpy as jnp
from jax import lax
from jax.experimental import pallas as pl
from jax.experimental.pallas import tpu as pltpu
from jax.sharding import PartitionSpec as P

HEAD = 128
GROUP = 16
FLEN = 128
SPAN = 8
TOK = 128
F32 = jnp.float32
BF16 = jnp.bfloat16


PLACES = ((0, 0), (0, 1), (2, 0), (1, 0), (1, 1), (3, 0), (3, 1), (2, 1))
LOADS = ((0,), (1, 2), (3, 4, 5, 6, 7))
LIMIT = 12 * 2**20
VMEM = pl.BlockSpec(memory_space=pltpu.VMEM)
FAR = pl.BlockSpec(memory_space=pl.ANY)


def call(body, out_shape, flops, moved, limit=None):
    one = not isinstance(out_shape, (list, tuple))
    return pl.pallas_call(
        body,
        out_shape=out_shape,
        out_specs=VMEM if one else [VMEM] * len(out_shape),
        compiler_params=pltpu.CompilerParams(vmem_limit_bytes=limit),
        cost_estimate=pl.CostEstimate(flops=flops, bytes_accessed=moved, transcendentals=0),
    )


def dot(a, b, ca=1, cb=0):
    return lax.dot_general(a, b, (((ca,), (cb,)), ((), ())), preferred_element_type=F32)


def onehot(ids_row, vocab):
    column = jnp.transpose(jnp.broadcast_to(ids_row, (TOK, TOK)))
    lane = lax.broadcasted_iota(jnp.int32, (TOK, TOK), 1)
    parts = [(column == lane + k * TOK).astype(F32).astype(BF16) for k in range(vocab // TOK)]
    return jnp.concatenate(parts, axis=1)


def place_of(k):
    along, flip = PLACES[k]
    tp = lax.axis_index("tp")
    return lax.rem(lax.div(tp, 2) + 4 - along, 4) * 2 + lax.rem(tp + flip, 2)


def load_weights(step, weight_hbm, weight_ref, sems):
    channels = weight_ref.shape[1]
    copies = []
    for j, k in enumerate(LOADS[step]):
        here = pl.ds(pl.multiple_of(place_of(k) * channels, channels), channels)
        copies.append(pltpu.make_async_copy(weight_hbm.at[here], weight_ref.at[j], sems.at[j]))
        copies[-1].start()
    return copies


def taps_body(ids_hbm, filters_hbm, table_hbm, weight_hbm, taps_ref, table_ref, ids_ref, weight_ref, filters_ref, sems, weight_sems):
    filters_copy = pltpu.make_async_copy(filters_hbm, filters_ref, sems.at[0])
    ids_copy = pltpu.make_async_copy(ids_hbm, ids_ref, sems.at[1])
    table_copy = pltpu.make_async_copy(table_hbm, table_ref, sems.at[2])
    filters_copy.start()
    ids_copy.start()
    table_copy.start()
    copies = load_weights(0, weight_hbm, weight_ref, weight_sems)
    row = lax.broadcasted_iota(jnp.int32, (FLEN, FLEN), 0)
    col = lax.broadcasted_iota(jnp.int32, (FLEN, FLEN), 1)
    flip = (((row + col) & (FLEN - 1)) == 0).astype(F32).astype(BF16)
    own = col <= row
    filters_copy.wait()
    taps = filters_ref[...]
    high = taps.astype(BF16)
    low = (taps - high.astype(F32)).astype(BF16)
    turned = dot(high, flip) + dot(low, flip)
    for g in range(taps.shape[0]):
        spread = jnp.broadcast_to(turned[g : g + 1], (FLEN, FLEN))
        circle = pltpu.roll(spread, 0, 1, stride=1, stride_axis=0)
        for part in range(2):
            rounded = circle.astype(BF16).astype(F32)
            base = part * 2 * FLEN
            taps_ref[g, :, base : base + FLEN] = jnp.where(own, 0.0, rounded).astype(BF16)
            taps_ref[g, :, base + FLEN : base + 2 * FLEN] = jnp.where(own, rounded, 0.0).astype(BF16)
            circle = circle - rounded
    for copy in [ids_copy, table_copy] + copies:
        copy.wait()


def gate_body(own_ref, before_ref, table_ref, taps_ref, gated_ref, pair_ref):
    pair_ref[0:1] = before_ref[...]
    pair_ref[1:2] = own_ref[...]
    width = table_ref.shape[2]
    vocab = table_ref.shape[1]
    here = onehot(own_ref[...], vocab)
    both = jnp.concatenate([onehot(before_ref[...], vocab), here], axis=0)
    mixed = dot(both, table_ref[1]) * dot(both, table_ref[2])
    row = lax.broadcasted_iota(jnp.int32, mixed.shape, 0)
    mixed = jnp.where((row >= TOK) | (lax.axis_index("ctx") > 0), mixed, 0.0).astype(BF16)
    post = dot(here, table_ref[0])
    lane_group = lax.broadcasted_iota(jnp.int32, (TOK, HEAD), 1) // GROUP
    per = HEAD // GROUP
    for part in range(width // HEAD):
        cols = slice(part * HEAD, (part + 1) * HEAD)
        window = jnp.concatenate([mixed[:, cols], mixed[:, cols]], axis=0)
        taps = taps_ref[part * per : (part + 1) * per].reshape(per * FLEN, 4 * FLEN)
        every = dot(taps, window)
        conv = every[:TOK]
        for g in range(1, per):
            conv = jnp.where(lane_group == g, every[g * TOK : (g + 1) * TOK], conv)
        gated_ref[:, cols] = (post[:, cols] * conv).astype(BF16)


def turn():
    row = lax.broadcasted_iota(jnp.int32, (FLEN, FLEN), 0)
    col = lax.broadcasted_iota(jnp.int32, (FLEN, FLEN), 1)
    return (((row + col) & (FLEN - 1)) == 0).astype(F32).astype(BF16)


def window_body(pair, k2, k4, k6, k8, near, table_ref, filters_hbm, value_ref, mixed_t, post_t, taps_ref, filters_ref, sem):
    filters_copy = pltpu.make_async_copy(filters_hbm, filters_ref, sem)
    filters_copy.start()
    vocab, width = table_ref.shape[1], table_ref.shape[2]
    position = lax.axis_index("ctx")

    def decode(key, k):
        code = (key if key.shape[0] == 8 else key[TOK:, :]).astype(F32)
        line, part = divmod(2 * k, 4)
        code = code[line : line + 1]
        return code[:, part * TOK : (part + 1) * TOK] * 16.0 + code[:, (part + 1) * TOK : (part + 2) * TOK]

    last = jnp.where(lax.rem(position, 2) == 1, decode(k8, 0), decode(near[2, TOK:, :], 1))
    rows = [last, decode(k6, 1), decode(k6, 0), decode(k4, 1), decode(k4, 0), decode(k2, 1), decode(k2, 0)]
    rows.append(pair[0:1].astype(F32))
    entry = lax.broadcasted_iota(jnp.int32, (vocab, 2 * TOK), 0).astype(F32)
    for n in range(0, SPAN, 2):
        ids = jnp.concatenate(rows[n : n + 2], axis=1)
        here = (entry == jnp.broadcast_to(ids, entry.shape)).astype(F32).astype(BF16)
        mixed = dot(table_ref[1], here, 0, 0) * dot(table_ref[2], here, 0, 0)
        lane = lax.broadcasted_iota(jnp.int32, mixed.shape, 1) // TOK
        mixed_t[:, n * TOK : (n + 2) * TOK] = jnp.where(position >= SPAN - n - lane, mixed, 0.0).astype(BF16)
        post_t[:, n * TOK : (n + 2) * TOK] = dot(table_ref[0], here, 0, 0).astype(BF16)
    filters_copy.wait()
    row = lax.broadcasted_iota(jnp.int32, (FLEN, FLEN), 0)
    col = lax.broadcasted_iota(jnp.int32, (FLEN, FLEN), 1)
    turned = dot(filters_ref[...].astype(BF16), turn())
    for g in range(taps_ref.shape[0]):
        circle = pltpu.roll(jnp.broadcast_to(turned[g : g + 1], (FLEN, FLEN)), 0, 1, stride=1, stride_axis=0)
        taps_ref[g, :, :FLEN] = jnp.where(col <= row, 0.0, circle).astype(BF16)
        taps_ref[g, :, FLEN:] = jnp.where(col <= row, circle, 0.0).astype(BF16)
    for g in range(width // GROUP):
        rows = slice(g * GROUP, (g + 1) * GROUP)
        windows = jnp.concatenate(
            [mixed_t[rows, n * TOK : (n + 2) * TOK] for n in range(SPAN - 1)], axis=0
        )
        conv = dot(windows, taps_ref[g], 1, 1)
        for n in range(SPAN - 1):
            post = post_t[rows, (n + 1) * TOK : (n + 2) * TOK].astype(F32)
            value_ref[SPAN - 2 - n, rows, :] = (post * conv[n * GROUP : (n + 1) * GROUP]).astype(BF16)


def term_of(piece, weight):
    channels = piece.shape[1]
    row = lax.broadcasted_iota(jnp.int32, (HEAD, 2 * HEAD), 0)
    col = lax.broadcasted_iota(jnp.int32, (HEAD, 2 * HEAD), 1)
    halves = []
    for which in range(2):
        place = (col == 2 * row + which).astype(F32).astype(BF16)
        parts = [dot(piece[:, j * HEAD : (j + 1) * HEAD], place).astype(BF16) for j in range(channels // HEAD)]
        halves.append(jnp.concatenate(parts, axis=1))
    return dot(jnp.concatenate(halves, axis=0), weight.reshape(2 * channels, weight.shape[2]))


def own_body(piece, own_weight, weight_hbm, weight_ref, total_ref, sems):
    copies = load_weights(1, weight_hbm, weight_ref, sems)
    total_ref[...] = term_of(piece[...], own_weight[0])
    for copy in copies:
        copy.wait()


def early_body(flipped, far, weight1, total_ref, weight_hbm, weight_ref, out_ref, sems):
    copies = load_weights(2, weight_hbm, weight_ref, sems)
    out_ref[...] = total_ref[...] + term_of(flipped[...], weight1[0]) + term_of(far[...], weight1[1])
    for copy in copies:
        copy.wait()


def project_body(chosen, last, *refs):
    count = len(chosen)
    arrays, weight_ref, total_ref, refs = refs[:count], refs[count], refs[count + 1], refs[count + 2 :]
    total = total_ref[...]
    for numbers, array in zip(chosen, arrays):
        for j, k in enumerate(numbers):
            piece = array[...] if len(numbers) == 1 else array[j]
            total = total + term_of(piece, weight_ref[LOADS[2].index(k)])
    if not last:
        refs[0][...] = total
        return
    pair_ref, query_ref, key_ref = refs
    rows, width = query_ref.shape
    query_ref[...] = total[:rows].astype(BF16)
    key_ref[:rows] = total[rows:].astype(BF16)
    ids = [pair_ref[1:2], pair_ref[0:1]]
    code = jnp.concatenate([part for row in ids for part in (row >> 4, row & 15)], axis=1).astype(F32)
    key_ref[rows:] = jnp.broadcast_to(code, (key_ref.shape[0] - rows, width)).astype(BF16)


def attend_body(query_ref, own_key, own_value, k2, k4, k6, near, near6, values, out_ref):
    position = lax.axis_index("ctx")
    odd = lax.rem(position, 2)
    far = [2, 4, 6, 1 + 2 * odd, 3 + 2 * odd, 7 - 6 * odd, 5 + 2 * odd]
    row = lax.broadcasted_iota(jnp.int32, (TOK, TOK), 0)
    col = lax.broadcasted_iota(jnp.int32, (TOK, TOK), 1)
    allowed = [col <= row] + [(col >= 0) & (position >= d) for d in far]
    allowed = jnp.concatenate([a.astype(F32) for a in allowed], axis=1) > 0.5
    for h in range(query_ref.shape[1] // HEAD):
        cols = slice(h * HEAD, (h + 1) * HEAD)
        keys = [key[:TOK, cols] for key in (own_key, k2, k4, k6)]
        keys += [near[j, :TOK, cols] for j in range(3)] + [near6[:TOK, cols]]
        scores = dot(query_ref[:, cols], jnp.concatenate(keys, axis=0), 1, 1) * HEAD ** (-0.5)
        scores = jnp.where(allowed, scores, -jnp.inf)
        largest = jnp.max(scores, axis=1, keepdims=True)
        weights = jnp.exp(scores - largest)
        row_sum = jnp.sum(weights, axis=1, keepdims=True)
        rounded = weights.astype(BF16)
        window = [values[d - 1, cols, :] for d in far]
        total = dot(rounded[:, :TOK], own_value[:, cols])
        total += dot(rounded[:, TOK:], jnp.concatenate(window, axis=1), 1, 1)
        out_ref[:, cols] = (total / row_sum).astype(BF16)


def behind(value, steps):
    count = lax.axis_size("ctx")
    return lax.ppermute(value, "ctx", [(s, s + steps) for s in range(count - steps)])


def shards(token_ids, stream_table, filters, proj_qk):
    width = stream_table.shape[2]
    groups = filters.shape[0]
    count = lax.axis_size("ctx")
    heads_axis = lax.axis_size("tp")
    shape = jax.ShapeDtypeStruct
    ids = token_ids.reshape(1, TOK)
    back1 = behind(ids, 1)
    weight_hbm = pltpu.with_memory_space_constraint(proj_qk, pltpu.MemorySpace.HBM)
    sizes = [shape((len(load), width) + proj_qk.shape[1:], BF16) for load in LOADS]
    sems = [pltpu.SemaphoreType.DMA((len(load),)) for load in LOADS]
    params = pltpu.CompilerParams(vmem_limit_bytes=LIMIT)
    taps, table, ids_near, weight0 = pl.pallas_call(
        taps_body,
        out_shape=[
            shape((groups, FLEN, 4 * FLEN), BF16), shape(stream_table.shape, BF16), shape(ids.shape, jnp.int32), sizes[0],
        ],
        in_specs=[FAR] * 4,
        out_specs=[VMEM] * 4,
        scratch_shapes=[pltpu.VMEM(filters.shape, F32), pltpu.SemaphoreType.DMA((3,)), sems[0]],
        compiler_params=params,
        cost_estimate=pl.CostEstimate(flops=10**8, bytes_accessed=4 * 2**20, transcendentals=0),
    )(*[pltpu.with_memory_space_constraint(a, pltpu.MemorySpace.HBM) for a in (ids, filters, stream_table)], weight_hbm)
    gated, pair = call(
        gate_body, [shape((TOK, width), BF16), shape((2, TOK), jnp.int32)], 10**9, 4 * 2**20, LIMIT
    )(ids_near, back1, table, taps)

    def spread(value, along, flip):
        route = [(s, (s // 2 + along) % 4 * 2 + (s + flip) % 2) for s in range(heads_axis)]
        return lax.ppermute(value, "tp", route)

    flipped = spread(gated, 0, 1)
    far = spread(gated, 2, 0)
    weight1, total = pl.pallas_call(
        own_body,
        out_shape=[sizes[1], shape((2 * TOK, width), F32)],
        in_specs=[VMEM, VMEM, FAR],
        out_specs=[VMEM] * 2,
        scratch_shapes=[sems[1]],
        compiler_params=params,
        cost_estimate=pl.CostEstimate(flops=10**9, bytes_accessed=2 * 2**20, transcendentals=0),
    )(gated, weight0, weight_hbm)
    flipped, total = lax.optimization_barrier((flipped, total))
    both = jnp.stack([gated, flipped])
    up = spread(both, 1, 0)
    down = spread(both, 3, 0)
    farflip = spread(flipped, 2, 0)
    weight2, total = pl.pallas_call(
        early_body,
        out_shape=[sizes[2], shape(total.shape, F32)],
        in_specs=[VMEM] * 4 + [FAR],
        out_specs=[VMEM] * 2,
        scratch_shapes=[sems[2]],
        compiler_params=params,
        cost_estimate=pl.CostEstimate(flops=2 * 10**9, bytes_accessed=5 * 2**20, transcendentals=0),
    )(flipped, far, weight1, total, weight_hbm)
    total = call(
        functools.partial(project_body, ((3, 4), (5, 6)), False), shape(total.shape, F32), 2 * 10**9, 2**20, LIMIT
    )(up, down, weight2, total)
    query, key = call(
        functools.partial(project_body, ((7,),), True),
        [shape((TOK, width), BF16), shape((TOK + 8, width), BF16)], 10**9, 2**20, LIMIT,
    )(farflip, weight2, total, pair)
    odd = lax.axis_index("ctx") % 2 == 1
    k4 = behind(key, 4)
    k2 = behind(key, 2)
    k8 = lax.ppermute(k4, "ctx", [(s, s + 4) for s in range(1, count - 4, 2)])
    k6 = behind(k4, 2)
    swap = [(s, s ^ 1) for s in range(count)]
    near = lax.ppermute(jnp.stack([k2, k4, jnp.where(odd, k8, key)]), "ctx", swap)
    near6 = lax.ppermute(k6, "ctx", swap)
    values = pl.pallas_call(
        window_body,
        out_shape=shape((SPAN - 1, width, TOK), BF16),
        in_specs=[VMEM] * 7 + [FAR],
        out_specs=VMEM,
        scratch_shapes=[
            pltpu.VMEM((width, SPAN * TOK), BF16), pltpu.VMEM((width, SPAN * TOK), BF16),
            pltpu.VMEM((groups, FLEN, 2 * FLEN), BF16), pltpu.VMEM(filters.shape, F32), pltpu.SemaphoreType.DMA,
        ],
        compiler_params=pltpu.CompilerParams(vmem_limit_bytes=LIMIT),
        cost_estimate=pl.CostEstimate(flops=2 * 10**9, bytes_accessed=6 * 2**20, transcendentals=0),
    )(pair, k2, k4, k6, k8, near, table, pltpu.with_memory_space_constraint(filters, pltpu.MemorySpace.HBM))
    return call(attend_body, shape((TOK, width), BF16), 10**9, 2 * 2**20, LIMIT)(
        query, key, gated, k2, k4, k6, near, near6, values
    )


def solution(mesh):
    placed = (P("ctx"), P(None, None, "tp"), P("tp", None), P(None, None, "tp"))

    return jax.shard_map(shards, mesh=mesh, in_specs=placed, out_specs=P("ctx", "tp"), check_vma=False)
```

```python
import functools

import jax
import jax.numpy as jnp
from jax import lax
from jax.experimental import pallas as pl
from jax.experimental.pallas import tpu as pltpu
from jax.sharding import PartitionSpec as P

HEAD = 128
GROUP = 16
FLEN = 128
SPAN = 8
TOK = 128
F32 = jnp.float32
BF16 = jnp.bfloat16


PLACES = ((0, 0), (0, 1), (2, 0), (1, 0), (1, 1), (3, 0), (3, 1), (2, 1))
LOADS = ((0,), (1, 2), (3, 4, 5, 6, 7))
LIMIT = 12 * 2**20
VMEM = pl.BlockSpec(memory_space=pltpu.VMEM)
FAR = pl.BlockSpec(memory_space=pl.ANY)


def call(body, out_shape, flops, moved, limit=None):
    one = not isinstance(out_shape, (list, tuple))
    return pl.pallas_call(
        body,
        out_shape=out_shape,
        out_specs=VMEM if one else [VMEM] * len(out_shape),
        compiler_params=pltpu.CompilerParams(vmem_limit_bytes=limit),
        cost_estimate=pl.CostEstimate(flops=flops, bytes_accessed=moved, transcendentals=0),
    )


def dot(a, b, ca=1, cb=0):
    return lax.dot_general(a, b, (((ca,), (cb,)), ((), ())), preferred_element_type=F32)


def onehot(ids_row, vocab):
    column = jnp.transpose(jnp.broadcast_to(ids_row, (TOK, TOK)))
    lane = lax.broadcasted_iota(jnp.int32, (TOK, TOK), 1)
    parts = [(column == lane + k * TOK).astype(F32).astype(BF16) for k in range(vocab // TOK)]
    return jnp.concatenate(parts, axis=1)


def place_of(k):
    along, flip = PLACES[k]
    tp = lax.axis_index("tp")
    return lax.rem(lax.div(tp, 2) + 4 - along, 4) * 2 + lax.rem(tp + flip, 2)


def load_weights(step, weight_hbm, weight_ref, sems):
    channels = weight_ref.shape[1]
    copies = []
    for j, k in enumerate(LOADS[step]):
        here = pl.ds(pl.multiple_of(place_of(k) * channels, channels), channels)
        copies.append(pltpu.make_async_copy(weight_hbm.at[here], weight_ref.at[j], sems.at[j]))
        copies[-1].start()
    return copies


def taps_body(ids_hbm, filters_hbm, table_hbm, weight_hbm, taps_ref, table_ref, ids_ref, weight_ref, filters_ref, sems, weight_sems):
    filters_copy = pltpu.make_async_copy(filters_hbm, filters_ref, sems.at[0])
    ids_copy = pltpu.make_async_copy(ids_hbm, ids_ref, sems.at[1])
    table_copy = pltpu.make_async_copy(table_hbm, table_ref, sems.at[2])
    filters_copy.start()
    ids_copy.start()
    table_copy.start()
    copies = load_weights(0, weight_hbm, weight_ref, weight_sems)
    row = lax.broadcasted_iota(jnp.int32, (FLEN, FLEN), 0)
    col = lax.broadcasted_iota(jnp.int32, (FLEN, FLEN), 1)
    flip = (((row + col) & (FLEN - 1)) == 0).astype(F32).astype(BF16)
    own = col <= row
    filters_copy.wait()
    taps = filters_ref[...]
    high = taps.astype(BF16)
    low = (taps - high.astype(F32)).astype(BF16)
    turned = dot(high, flip) + dot(low, flip)
    for g in range(taps.shape[0]):
        spread = jnp.broadcast_to(turned[g : g + 1], (FLEN, FLEN))
        circle = pltpu.roll(spread, 0, 1, stride=1, stride_axis=0)
        for part in range(2):
            rounded = circle.astype(BF16).astype(F32)
            base = part * 2 * FLEN
            taps_ref[g, :, base : base + FLEN] = jnp.where(own, 0.0, rounded).astype(BF16)
            taps_ref[g, :, base + FLEN : base + 2 * FLEN] = jnp.where(own, rounded, 0.0).astype(BF16)
            circle = circle - rounded
    for copy in [ids_copy, table_copy] + copies:
        copy.wait()


def gate_body(own_ref, before_ref, table_ref, taps_ref, gated_ref, pair_ref):
    pair_ref[0:1] = before_ref[...]
    pair_ref[1:2] = own_ref[...]
    width = table_ref.shape[2]
    vocab = table_ref.shape[1]
    here = onehot(own_ref[...], vocab)
    both = jnp.concatenate([onehot(before_ref[...], vocab), here], axis=0)
    mixed = dot(both, table_ref[1]) * dot(both, table_ref[2])
    row = lax.broadcasted_iota(jnp.int32, mixed.shape, 0)
    mixed = jnp.where((row >= TOK) | (lax.axis_index("ctx") > 0), mixed, 0.0).astype(BF16)
    post = dot(here, table_ref[0])
    lane_group = lax.broadcasted_iota(jnp.int32, (TOK, HEAD), 1) // GROUP
    per = HEAD // GROUP
    for part in range(width // HEAD):
        cols = slice(part * HEAD, (part + 1) * HEAD)
        window = jnp.concatenate([mixed[:, cols], mixed[:, cols]], axis=0)
        taps = taps_ref[part * per : (part + 1) * per].reshape(per * FLEN, 4 * FLEN)
        every = dot(taps, window)
        conv = every[:TOK]
        for g in range(1, per):
            conv = jnp.where(lane_group == g, every[g * TOK : (g + 1) * TOK], conv)
        gated_ref[:, cols] = (post[:, cols] * conv).astype(BF16)


def turn():
    row = lax.broadcasted_iota(jnp.int32, (FLEN, FLEN), 0)
    col = lax.broadcasted_iota(jnp.int32, (FLEN, FLEN), 1)
    return (((row + col) & (FLEN - 1)) == 0).astype(F32).astype(BF16)


def decode(tail, before):
    code = tail.astype(F32)[:1, before * 2 * TOK : (before + 1) * 2 * TOK]
    return code[:, :TOK] * 16.0 + code[:, TOK:]


def window_values(rows, nearest, table_ref, taps_ref, value_ref, mixed_t, post_t, prepare=None):
    vocab, width = table_ref.shape[1], table_ref.shape[2]
    many = len(rows) - 1
    position = lax.axis_index("ctx")
    entry = lax.broadcasted_iota(jnp.int32, (vocab, TOK), 0).astype(F32)
    here = [(entry == jnp.broadcast_to(row, entry.shape)).astype(F32).astype(BF16) for row in rows]
    every = jnp.concatenate(here, axis=1)
    mixed = dot(table_ref[1], every, 0, 0) * dot(table_ref[2], every, 0, 0)
    for n in range(many + 1):
        part = mixed[:, n * TOK : (n + 1) * TOK]
        mixed_t[:, n * TOK : (n + 1) * TOK] = jnp.where(position >= nearest + many - n, part, 0.0).astype(BF16)
    post_t[...] = dot(table_ref[0], jnp.concatenate(here[1:], axis=1), 0, 0).astype(BF16)
    if prepare is not None:
        prepare()
    for g in range(width // GROUP):
        rows = slice(g * GROUP, (g + 1) * GROUP)
        windows = jnp.concatenate([mixed_t[rows, n * TOK : (n + 2) * TOK] for n in range(many)], axis=0)
        conv = dot(windows, taps_ref[g], 1, 1)
        for n in range(many):
            post = post_t[rows, n * TOK : (n + 1) * TOK].astype(F32)
            value_ref[many - 1 - n, rows, :] = (post * conv[n * GROUP : (n + 1) * GROUP]).astype(BF16)


def near_body(pair, k2, k4, table, filters_hbm, value_ref, taps_ref, mixed_t, post_t, filters_ref, sem):
    filters_copy = pltpu.make_async_copy(filters_hbm, filters_ref, sem)
    filters_copy.start()

    def prepare():
        filters_copy.wait()
        row = lax.broadcasted_iota(jnp.int32, (FLEN, FLEN), 0)
        col = lax.broadcasted_iota(jnp.int32, (FLEN, FLEN), 1)
        turned = dot(filters_ref[...].astype(BF16), turn())
        for g in range(taps_ref.shape[0]):
            circle = pltpu.roll(jnp.broadcast_to(turned[g : g + 1], (FLEN, FLEN)), 0, 1, stride=1, stride_axis=0)
            taps_ref[g, :, :FLEN] = jnp.where(col <= row, 0.0, circle).astype(BF16)
            taps_ref[g, :, FLEN:] = jnp.where(col <= row, circle, 0.0).astype(BF16)

    rows = [decode(k4[TOK:, :], 1), decode(k4[TOK:, :], 0), decode(k2[TOK:, :], 1), decode(k2[TOK:, :], 0)]
    window_values(rows + [pair[0:1].astype(F32)], 1, table, taps_ref, value_ref, mixed_t, post_t, prepare)


def far_body(k4, k6, k8, near, table, taps, value_ref, mixed_t, post_t):
    odd = lax.rem(lax.axis_index("ctx"), 2) == 1
    last = jnp.where(odd, decode(k8[TOK:, :], 0), decode(near[2, TOK:, :], 1))
    rows = [last, decode(k6[TOK:, :], 1), decode(k6[TOK:, :], 0), decode(k4[TOK:, :], 1)]
    window_values(rows, 5, table, taps, value_ref, mixed_t, post_t)


def term_of(piece, weight):
    channels = piece.shape[1]
    row = lax.broadcasted_iota(jnp.int32, (HEAD, 2 * HEAD), 0)
    col = lax.broadcasted_iota(jnp.int32, (HEAD, 2 * HEAD), 1)
    halves = []
    for which in range(2):
        place = (col == 2 * row + which).astype(F32).astype(BF16)
        parts = [dot(piece[:, j * HEAD : (j + 1) * HEAD], place).astype(BF16) for j in range(channels // HEAD)]
        halves.append(jnp.concatenate(parts, axis=1))
    return dot(jnp.concatenate(halves, axis=0), weight.reshape(2 * channels, weight.shape[2]))


def own_body(piece, own_weight, weight_hbm, weight_ref, total_ref, sems):
    copies = load_weights(1, weight_hbm, weight_ref, sems)
    total_ref[...] = term_of(piece[...], own_weight[0])
    for copy in copies:
        copy.wait()


def early_body(flipped, far, weight1, total_ref, weight_hbm, weight_ref, out_ref, sems):
    copies = load_weights(2, weight_hbm, weight_ref, sems)
    out_ref[...] = total_ref[...] + term_of(flipped[...], weight1[0]) + term_of(far[...], weight1[1])
    for copy in copies:
        copy.wait()


def project_body(chosen, last, *refs):
    count = len(chosen)
    arrays, weight_ref, total_ref, refs = refs[:count], refs[count], refs[count + 1], refs[count + 2 :]
    total = total_ref[...]
    for numbers, array in zip(chosen, arrays):
        for j, k in enumerate(numbers):
            piece = array[...] if len(numbers) == 1 else array[j]
            total = total + term_of(piece, weight_ref[LOADS[2].index(k)])
    if not last:
        refs[0][...] = total
        return
    pair_ref, query_ref, key_ref = refs
    rows, width = query_ref.shape
    query_ref[...] = total[:rows].astype(BF16)
    key_ref[:rows] = total[rows:].astype(BF16)
    ids = [pair_ref[1:2], pair_ref[0:1]]
    code = jnp.concatenate([part for row in ids for part in (row >> 4, row & 15)], axis=1).astype(F32)
    key_ref[rows:] = jnp.broadcast_to(code, (key_ref.shape[0] - rows, width)).astype(BF16)


def attend_body(query_ref, own_key, own_value, k2, k4, k6, near, near6, near_values, far_values, out_ref, values):
    position = lax.axis_index("ctx")
    odd = lax.rem(position, 2)
    far = [2, 4, 6, 1 + 2 * odd, 3 + 2 * odd, 7 - 6 * odd, 5 + 2 * odd]
    values[:4] = near_values[...]
    values[4:] = far_values[...]
    row = lax.broadcasted_iota(jnp.int32, (TOK, TOK), 0)
    col = lax.broadcasted_iota(jnp.int32, (TOK, TOK), 1)
    allowed = [col <= row] + [(col >= 0) & (position >= d) for d in far]
    allowed = jnp.concatenate([a.astype(F32) for a in allowed], axis=1) > 0.5
    for h in range(query_ref.shape[1] // HEAD):
        cols = slice(h * HEAD, (h + 1) * HEAD)
        keys = [key[:TOK, cols] for key in (own_key, k2, k4, k6)]
        keys += [near[j, :TOK, cols] for j in range(3)] + [near6[:TOK, cols]]
        scores = dot(query_ref[:, cols], jnp.concatenate(keys, axis=0), 1, 1) * HEAD ** (-0.5)
        scores = jnp.where(allowed, scores, -jnp.inf)
        largest = jnp.max(scores, axis=1, keepdims=True)
        weights = jnp.exp(scores - largest)
        row_sum = jnp.sum(weights, axis=1, keepdims=True)
        rounded = weights.astype(BF16)
        window = [values[d - 1, cols, :] for d in far]
        total = dot(rounded[:, :TOK], own_value[:, cols])
        total += dot(rounded[:, TOK:], jnp.concatenate(window, axis=1), 1, 1)
        out_ref[:, cols] = (total / row_sum).astype(BF16)


def behind(value, steps):
    count = lax.axis_size("ctx")
    return lax.ppermute(value, "ctx", [(s, s + steps) for s in range(count - steps)])


def shards(token_ids, stream_table, filters, proj_qk):
    width = stream_table.shape[2]
    groups = filters.shape[0]
    count = lax.axis_size("ctx")
    heads_axis = lax.axis_size("tp")
    shape = jax.ShapeDtypeStruct
    ids = token_ids.reshape(1, TOK)
    back1 = behind(ids, 1)
    weight_hbm = pltpu.with_memory_space_constraint(proj_qk, pltpu.MemorySpace.HBM)
    sizes = [shape((len(load), width) + proj_qk.shape[1:], BF16) for load in LOADS]
    sems = [pltpu.SemaphoreType.DMA((len(load),)) for load in LOADS]
    params = pltpu.CompilerParams(vmem_limit_bytes=LIMIT)
    taps, table, ids_near, weight0 = pl.pallas_call(
        taps_body,
        out_shape=[
            shape((groups, FLEN, 4 * FLEN), BF16), shape(stream_table.shape, BF16), shape(ids.shape, jnp.int32), sizes[0],
        ],
        in_specs=[FAR] * 4,
        out_specs=[VMEM] * 4,
        scratch_shapes=[pltpu.VMEM(filters.shape, F32), pltpu.SemaphoreType.DMA((3,)), sems[0]],
        compiler_params=params,
        cost_estimate=pl.CostEstimate(flops=10**8, bytes_accessed=4 * 2**20, transcendentals=0),
    )(*[pltpu.with_memory_space_constraint(a, pltpu.MemorySpace.HBM) for a in (ids, filters, stream_table)], weight_hbm)
    gated, pair = call(
        gate_body, [shape((TOK, width), BF16), shape((2, TOK), jnp.int32)], 10**9, 4 * 2**20, LIMIT
    )(ids_near, back1, table, taps)

    def spread(value, along, flip):
        route = [(s, (s // 2 + along) % 4 * 2 + (s + flip) % 2) for s in range(heads_axis)]
        return lax.ppermute(value, "tp", route)

    flipped = spread(gated, 0, 1)
    far = spread(gated, 2, 0)
    weight1, total = pl.pallas_call(
        own_body,
        out_shape=[sizes[1], shape((2 * TOK, width), F32)],
        in_specs=[VMEM, VMEM, FAR],
        out_specs=[VMEM] * 2,
        scratch_shapes=[sems[1]],
        compiler_params=params,
        cost_estimate=pl.CostEstimate(flops=10**9, bytes_accessed=2 * 2**20, transcendentals=0),
    )(gated, weight0, weight_hbm)
    flipped, total = lax.optimization_barrier((flipped, total))
    both = jnp.stack([gated, flipped])
    up = spread(both, 1, 0)
    down = spread(both, 3, 0)
    farflip = spread(far, 0, 1)
    weight2, total = pl.pallas_call(
        early_body,
        out_shape=[sizes[2], shape(total.shape, F32)],
        in_specs=[VMEM] * 4 + [FAR],
        out_specs=[VMEM] * 2,
        scratch_shapes=[sems[2]],
        compiler_params=params,
        cost_estimate=pl.CostEstimate(flops=2 * 10**9, bytes_accessed=5 * 2**20, transcendentals=0),
    )(flipped, far, weight1, total, weight_hbm)
    total = call(
        functools.partial(project_body, ((3, 4), (5, 6)), False), shape(total.shape, F32), 2 * 10**9, 2**20, LIMIT
    )(up, down, weight2, total)
    query, key = call(
        functools.partial(project_body, ((7,),), True),
        [shape((TOK, width), BF16), shape((TOK + 8, width), BF16)], 10**9, 2**20, LIMIT,
    )(farflip, weight2, total, pair)
    odd = lax.axis_index("ctx") % 2 == 1
    k4 = behind(key, 4)
    k2 = behind(key, 2)
    k8 = lax.ppermute(k4, "ctx", [(s, s + 4) for s in range(1, count - 4, 2)])
    k6 = behind(k2, 4)
    swap = [(s, s ^ 1) for s in range(count)]
    near = lax.ppermute(jnp.stack([k2, k4, jnp.where(odd, k8, key)]), "ctx", swap)
    near6 = lax.ppermute(k6, "ctx", swap)
    near_values, high = pl.pallas_call(
        near_body,
        out_shape=[shape((4, width, TOK), BF16), shape((groups, FLEN, 2 * FLEN), BF16)],
        in_specs=[VMEM] * 4 + [FAR],
        out_specs=[VMEM] * 2,
        scratch_shapes=[
            pltpu.VMEM((width, 5 * TOK), BF16), pltpu.VMEM((width, 4 * TOK), BF16),
            pltpu.VMEM(filters.shape, F32), pltpu.SemaphoreType.DMA,
        ],
        compiler_params=params,
        cost_estimate=pl.CostEstimate(flops=3 * 10**9, bytes_accessed=6 * 2**20, transcendentals=0),
    )(pair, k2, k4, table, pltpu.with_memory_space_constraint(filters, pltpu.MemorySpace.HBM))
    far_values = pl.pallas_call(
        far_body,
        out_shape=shape((3, width, TOK), BF16),
        out_specs=VMEM,
        scratch_shapes=[pltpu.VMEM((width, 4 * TOK), BF16), pltpu.VMEM((width, 3 * TOK), BF16)],
        compiler_params=params,
        cost_estimate=pl.CostEstimate(flops=2 * 10**9, bytes_accessed=6 * 2**20, transcendentals=0),
    )(k4, k6, k8, near, table, high)
    return pl.pallas_call(
        attend_body,
        out_shape=shape((TOK, width), BF16),
        out_specs=VMEM,
        scratch_shapes=[pltpu.VMEM((SPAN - 1, width, TOK), BF16)],
        compiler_params=params,
        cost_estimate=pl.CostEstimate(flops=10**9, bytes_accessed=6 * 2**20, transcendentals=0),
    )(query, key, gated, k2, k4, k6, near, near6, near_values, far_values)


def solution(mesh):
    placed = (P("ctx"), P(None, None, "tp"), P("tp", None), P(None, None, "tp"))

    return jax.shard_map(shards, mesh=mesh, in_specs=placed, out_specs=P("ctx", "tp"), check_vma=False)
```
